32 devices in a mesh: tp: 4 (over y, x), grp: 8 (over z, core).
Axes of the slice: x: 2, y: 2, z: 4, core: 2. Of those that a mesh axis runs over, the one named last changes fastest.
Arguments:
- low_feats: bfloat16 [384, 16384], P('grp', 'tp'), may hold values from -40 to 40
- mid_feats: bfloat16 [384, 16384], P('grp', 'tp'), may hold values from -40 to 40
- high_feats: bfloat16 [384, 16384], P('grp', 'tp'), may hold values from -40 to 40
- w_low: bfloat16 [16384, 16384], P('tp', 'grp'), may hold values from -3 to 3
- w_mid: bfloat16 [16384, 16384], P('tp', 'grp'), may hold values from -3 to 3
- w_high: bfloat16 [16384, 16384], P('tp', 'grp'), may hold values from -3 to 3
- norm_gain: float32 [16384], P('grp'), may hold values from 0.1 to 1.9
- accepted: int32 [64], replicated, may hold values from 0 to 5, as said below
- assignment: int32 [64], replicated, may hold values from 0 to 63, each once
Outputs:
- drafted: bfloat16 [384, 16384], P('tp', 'grp')
The draws below stay inside these ranges and needn't reach their ends.
Inputs may be any that keep to these rules, and one draw needn't show every extreme that they name: For every group of 8 consecutive rows starting at a multiple of 8, the sum of accepted + 1 is at most 32, and some group reaches 32; rows 2i and 2i+1 together have at most 8 positions with p <= accepted. `assignment`: each row appears once.
All inputs are finite; a program needn't handle non-finite values.
Results may differ from the reference program's by a relative error of at most 0.0008.
Values may be sent and summed in bfloat16 or wider, within the bound.
A program may use at most 128 MiB of HBM per device.

```python
import math
import jax
import jax.numpy as jnp
from jax import lax

D = 16384
ROWS_G = 8
POS = 6
ROWS = 64
TOKENS = 384


def feature_draw(key):
    key_rows, key_vals = jax.random.split(key, 2)
    row_scale = jnp.exp(jax.random.uniform(key_rows, (TOKENS, 1), jnp.float32, 0.0, math.log(10.0)))
    values = jax.random.normal(key_vals, (TOKENS, D), jnp.float32)
    values = jnp.clip(values, -4.0, 4.0)
    return (values * row_scale).astype(jnp.bfloat16)


def weight_draw(key):
    key_cols, key_vals = jax.random.split(key, 2)
    columns = jnp.arange(D, dtype=jnp.float32)
    col_scale = jnp.exp(math.log(3.0) * columns / D)[None, :]
    col_scale = col_scale * jnp.exp(jax.random.uniform(key_cols, (1, D), jnp.float32, 0.0, math.log(3.3)))
    values = jnp.clip(jax.random.normal(key_vals, (D, D), jnp.float32), -4.0, 4.0)
    return (values * col_scale * (0.5 / math.sqrt(D))).astype(jnp.bfloat16)


def draw_low_feats(key, part):
    return feature_draw(jax.random.fold_in(key, 11))


def draw_mid_feats(key, part):
    return feature_draw(jax.random.fold_in(key, 12))


def draw_high_feats(key, part):
    return feature_draw(jax.random.fold_in(key, 13))


def draw_w_low(key, part):
    return weight_draw(jax.random.fold_in(key, 21))


def draw_w_mid(key, part):
    return weight_draw(jax.random.fold_in(key, 22))


def draw_w_high(key, part):
    return weight_draw(jax.random.fold_in(key, 23))


def draw_accepted(key, part):
    key_upper, key_full, key_sums, key_split = jax.random.split(jax.random.fold_in(key, 31), 4)
    groups = ROWS // ROWS_G
    pairs = ROWS_G // 2
    group_index = jnp.arange(groups, dtype=jnp.int32)[:, None]
    upper = jax.random.randint(key_upper, (groups, 1), 2, 9)
    full_group = jax.random.randint(key_full, (), 0, groups)
    upper = jnp.where(group_index == full_group, 8, upper)
    lower = jnp.where(group_index == full_group, 8, 2)
    pair_sum = jax.random.randint(key_sums, (groups, pairs), lower, upper + 1)
    first_low = jnp.maximum(1, pair_sum - 6)
    first_high = jnp.minimum(6, pair_sum - 1)
    raw_bits = jax.random.randint(key_split, (groups, pairs), 0, 1 << 20)
    first = first_low + raw_bits % (first_high - first_low + 1)
    second = pair_sum - first
    used = jnp.stack([first, second], axis=-1).reshape(ROWS)
    return (used - 1).astype(jnp.int32)


def setup_inputs(seed: int = 0) -> dict:
    key_list = jax.random.split(jax.random.key(seed), 10)
    low_feats = draw_low_feats(jax.random.fold_in(key_list[9], 71), 0)
    mid_feats = draw_mid_feats(jax.random.fold_in(key_list[9], 71), 0)
    high_feats = draw_high_feats(jax.random.fold_in(key_list[9], 71), 0)
    w_low = draw_w_low(jax.random.fold_in(key_list[9], 71), 0)
    w_mid = draw_w_mid(jax.random.fold_in(key_list[9], 71), 0)
    w_high = draw_w_high(jax.random.fold_in(key_list[9], 71), 0)
    norm_gain = jnp.clip(1.0 + 0.18 * jax.random.normal(key_list[6], (D,), jnp.float32), 0.1, 1.9)
    accepted = draw_accepted(jax.random.fold_in(key_list[9], 71), 0)
    assignment = jax.random.permutation(key_list[8], ROWS).astype(jnp.int32)
    return dict(low_feats=low_feats, mid_feats=mid_feats, high_feats=high_feats, w_low=w_low, w_mid=w_mid, w_high=w_high, norm_gain=norm_gain, accepted=accepted, assignment=assignment)


EPSILON = 1e-05

def reference(low_feats, mid_feats, high_feats, w_low, w_mid, w_high, norm_gain, accepted, assignment):
    joined_rows = jnp.dot(low_feats, w_low, preferred_element_type=jnp.float32)
    joined_rows = joined_rows + jnp.dot(mid_feats, w_mid, preferred_element_type=jnp.float32)
    joined_rows = joined_rows + jnp.dot(high_feats, w_high, preferred_element_type=jnp.float32)
    total_tokens = accepted.shape[0] * POS
    step_index = jnp.arange(POS, dtype=jnp.int32)
    source_rows = (assignment[:, None] * POS + step_index[None, :]).reshape(total_tokens).astype(jnp.int32)
    live_rows = (step_index[None, :] <= accepted[assignment][:, None]).reshape(total_tokens)
    ordered = joined_rows[source_rows]
    squares = lax.optimization_barrier(jnp.sum(ordered * ordered, axis=1, keepdims=True))
    normed = ordered * lax.rsqrt(squares / D + EPSILON) * norm_gain[None, :]
    return jnp.where(live_rows[:, None], normed, jnp.zeros_like(normed)).astype(jnp.bfloat16)
```

```python
import functools

import jax
import jax.numpy as jnp
from jax import lax
from jax.experimental import pallas as pl
from jax.experimental.pallas import tpu as pltpu
from jax.sharding import PartitionSpec as P

ROWS_G = 8
POS = 6
CAPACITY = 4 * ROWS_G
BATCHES = 2
SLOTS = CAPACITY // BATCHES
LAYERS = 3
STEPS = BATCHES * LAYERS
AHEAD = 2
TILE = 256
EPSILON = 1e-05


def kernel(
    groups, owners,
    low_ref, mid_ref, high_ref, w_low, w_mid, w_high, gain_ref, pack_ref, pick_ref,
    out_ref,
    weights, blocks, sums, parts, squares, rows_out,
    w_sem, send_sem, recv_sem, part_send, part_recv, sq_send, sq_recv, row_send, row_recv,
):
    me = lax.axis_index("grp")
    own = lax.axis_index("tp")
    chip, core = me // 2, me % 2
    chips = groups // 2
    sibling = chip * 2 + 1 - core
    columns = sums.shape[2]
    share = rows_out.shape[2]
    width = groups * columns

    loads = [
        pltpu.make_async_copy(w, weights.at[i], w_sem.at[i])
        for i, w in enumerate((w_low, w_mid, w_high))
    ]
    for load in loads:
        load.start()

    barrier = pltpu.get_barrier_semaphore()
    for d in range(1, groups):
        pl.semaphore_signal(
            barrier, inc=1, device_id={"grp": lax.rem(me + d, groups)},
            device_id_type=pl.DeviceIdType.MESH,
        )
    for d in range(1, owners):
        pl.semaphore_signal(
            barrier, inc=1, device_id={"tp": lax.rem(own + d, owners)},
            device_id_type=pl.DeviceIdType.MESH,
        )

    def rows_of(group):
        return pl.ds(pl.multiple_of(group * SLOTS, SLOTS), SLOTS)

    for i, feats in enumerate((low_ref, mid_ref, high_ref)):
        packed = jnp.dot(
            pack_ref[...], feats[...], preferred_element_type=jnp.float32
        ).astype(jnp.bfloat16)
        for b in range(BATCHES):
            blocks[b * LAYERS + i, rows_of(me), :] = packed[b * SLOTS : (b + 1) * SLOTS]

    pl.semaphore_wait(barrier, groups + owners - 2)

    def block_copy(way, step, group):
        target = (chip * 2 + 2 + core, chip * 2 - 2 + core, sibling)[way]
        return pltpu.make_async_remote_copy(
            src_ref=blocks.at[step, rows_of(group), :],
            dst_ref=blocks.at[step, rows_of(group), :],
            send_sem=send_sem.at[way, step, group // 2],
            recv_sem=recv_sem.at[step, group],
            device_id={"grp": target},
            device_id_type=pl.DeviceIdType.MESH,
        )

    def send_own(step):
        @pl.when(chip < chips - 1)
        def _():
            block_copy(0, step, me).start()

        @pl.when(chip > 0)
        def _():
            block_copy(1, step, me).start()

        block_copy(2, step, me).start()

    def relay(step):
        for d in range(1, chips):
            @pl.when(chip - d >= 0)
            def _():
                group = me - 2 * d
                block_copy(0, step, group).wait_recv()

                @pl.when(chip < chips - 1)
                def _():
                    block_copy(0, step, group).start()

                block_copy(2, step, group).start()

            @pl.when(chip + d <= chips - 1)
            def _():
                group = me + 2 * d
                block_copy(1, step, group).wait_recv()

                @pl.when(chip > 0)
                def _():
                    block_copy(1, step, group).start()

                block_copy(2, step, group).start()
        for q in range(chips):
            block_copy(2, step, q * 2 + 1 - core).wait_recv()

    def multiply(step):
        b, layer = step // LAYERS, step % LAYERS

        @pl.loop(0, columns // TILE)
        def _(j):
            cols = pl.ds(pl.multiple_of(j * TILE, TILE), TILE)
            product = jnp.dot(
                blocks[step], weights[layer, :, cols], preferred_element_type=jnp.float32
            )
            if layer == 0:
                sums[b, :, cols] = product
            else:
                sums[b, :, cols] += product

    def share_of(owner):
        return pl.ds(pl.multiple_of(owner * share, share), share)

    def part_copy(b, d):
        target = lax.rem(own + d, owners)
        return pltpu.make_async_remote_copy(
            src_ref=sums.at[b, share_of(target), :],
            dst_ref=parts.at[b, d - 1],
            send_sem=part_send.at[b, d - 1],
            recv_sem=part_recv.at[b, d - 1],
            device_id={"tp": target},
            device_id_type=pl.DeviceIdType.MESH,
        )

    def square_copy(b, d):
        return pltpu.make_async_remote_copy(
            src_ref=squares.at[b, 0],
            dst_ref=squares.at[b, d],
            send_sem=sq_send.at[b, d - 1],
            recv_sem=sq_recv.at[b, d - 1],
            device_id={"grp": lax.rem(me + d, groups)},
            device_id_type=pl.DeviceIdType.MESH,
        )

    def row_copy(b, d):
        return pltpu.make_async_remote_copy(
            src_ref=rows_out.at[b, own],
            dst_ref=rows_out.at[b, own],
            send_sem=row_send.at[b, d - 1],
            recv_sem=row_recv.at[b, d - 1],
            device_id={"tp": lax.rem(own + d, owners)},
            device_id_type=pl.DeviceIdType.MESH,
        )

    diagonal = lax.broadcasted_iota(jnp.int32, (share, 128), 0) == lax.broadcasted_iota(
        jnp.int32, (share, 128), 1
    )

    def spread(b):
        for d in range(1, owners):
            part_copy(b, d).start()

    def reduce(b):
        total = sums[b, share_of(own), :]
        for d in range(1, owners):
            part_copy(b, d).wait_recv()
            total = total + parts[b, d - 1]
        parts[b, owners - 1] = total
        square = jnp.sum(total * total, axis=1, keepdims=True)
        lanes = jnp.sum(jnp.where(diagonal, square, 0.0), axis=0, keepdims=True)
        squares[b, 0] = jnp.broadcast_to(lanes, (8, 128))
        for d in range(1, groups):
            square_copy(b, d).start()

    def finish(b):
        for d in range(1, groups):
            square_copy(b, d).wait_recv()
        lanes = squares[b, 0]
        for d in range(1, groups):
            lanes = lanes + squares[b, d]
        square = jnp.sum(jnp.where(diagonal, lanes[0:1], 0.0), axis=1, keepdims=True)
        inverse = lax.rsqrt(square / width + EPSILON)
        rows_out[b, own] = (parts[b, owners - 1] * inverse * gain_ref[...]).astype(jnp.bfloat16)
        for d in range(1, owners):
            row_copy(b, d).start()

    for step in range(AHEAD):
        send_own(step)
    for step in range(STEPS):
        if step + AHEAD < STEPS:
            send_own(step + AHEAD)
        relay(step)
        if step < LAYERS:
            loads[step].wait()
        multiply(step)
        if step % LAYERS == LAYERS - 1:
            spread(step // LAYERS)
        if step >= LAYERS and step % LAYERS == 0:
            reduce(step // LAYERS - 1)
        if step >= LAYERS and step % LAYERS == 1:
            finish(step // LAYERS - 1)
    reduce(BATCHES - 1)
    finish(BATCHES - 1)
    for b in range(BATCHES):
        for d in range(1, owners):
            row_copy(b, d).wait_recv()

    everything = rows_out[...].reshape(BATCHES * owners * share, columns)
    out_ref[...] = jnp.dot(
        pick_ref[...], everything, preferred_element_type=jnp.float32
    ).astype(jnp.bfloat16)

    for step in range(STEPS):
        for q in range(chips):
            group = q * 2 + core

            @pl.when((chip < chips - 1) & (q <= chip))
            def _():
                block_copy(0, step, group).wait_send()

            @pl.when((chip > 0) & (q >= chip))
            def _():
                block_copy(1, step, group).wait_send()

            block_copy(2, step, group).wait_send()
    for b in range(BATCHES):
        for d in range(1, owners):
            part_copy(b, d).wait_send()
            row_copy(b, d).wait_send()
        for d in range(1, groups):
            square_copy(b, d).wait_send()


def per_device(
    groups, owners,
    low_feats, mid_feats, high_feats, w_low, w_mid, w_high, norm_gain, accepted, assignment,
):
    tokens, depth = low_feats.shape
    columns = w_low.shape[1]
    rows = accepted.shape[0]
    batch_rows = groups * SLOTS
    share = batch_rows // owners
    slab = rows * POS // owners

    row = jnp.arange(rows, dtype=jnp.int32)
    position = jnp.arange(POS, dtype=jnp.int32)
    before = jnp.where(row % 2 == 1, jnp.roll(accepted, 1) + 1, 0)
    local = row % ROWS_G
    first_slot = (local // 2) * (2 * CAPACITY // ROWS_G) + before
    slot = first_slot[:, None] + position[None, :]
    live = position[None, :] <= accepted[:, None]
    slot = jnp.where(live, slot, -1)
    me = lax.axis_index("grp")
    own_slot = lax.dynamic_slice_in_dim(slot, me * ROWS_G, ROWS_G).reshape(tokens)
    pack = (jnp.arange(CAPACITY, dtype=jnp.int32)[:, None] == own_slot[None, :]).astype(
        jnp.bfloat16
    )
    place = jnp.where(
        live,
        (slot // SLOTS) * batch_rows + (row // ROWS_G)[:, None] * SLOTS + slot % SLOTS,
        -1,
    )
    own_assignment = lax.dynamic_slice_in_dim(
        assignment, lax.axis_index("tp") * (rows // owners), rows // owners
    )
    taken = own_assignment[:, None] == row[None, :]
    own_place = jnp.sum(jnp.where(taken[:, :, None], place[None], 0), axis=1).reshape(slab)
    pick = (
        own_place[:, None] == jnp.arange(BATCHES * batch_rows, dtype=jnp.int32)[None, :]
    ).astype(jnp.bfloat16)

    vmem = pl.BlockSpec(memory_space=pltpu.VMEM)
    hbm = pl.BlockSpec(memory_space=pl.ANY)
    dma = pltpu.SemaphoreType.DMA
    return pl.pallas_call(
        functools.partial(kernel, groups, owners),
        out_shape=jax.ShapeDtypeStruct((slab, columns), jnp.bfloat16),
        in_specs=[vmem] * 3 + [hbm] * 3 + [vmem] * 3,
        out_specs=vmem,
        scratch_shapes=[
            pltpu.VMEM((LAYERS, depth, columns), jnp.bfloat16),
            pltpu.VMEM((STEPS, batch_rows, depth), jnp.bfloat16),
            pltpu.VMEM((BATCHES, batch_rows, columns), jnp.float32),
            pltpu.VMEM((BATCHES, owners, share, columns), jnp.float32),
            pltpu.VMEM((BATCHES, groups, 8, 128), jnp.float32),
            pltpu.VMEM((BATCHES, owners, share, columns), jnp.bfloat16),
            dma((LAYERS,)),
            dma((3, STEPS, groups // 2)),
            dma((STEPS, groups)),
            dma((BATCHES, owners - 1)),
            dma((BATCHES, owners - 1)),
            dma((BATCHES, groups - 1)),
            dma((BATCHES, groups - 1)),
            dma((BATCHES, owners - 1)),
            dma((BATCHES, owners - 1)),
        ],
        compiler_params=pltpu.CompilerParams(
            collective_id=0, has_side_effects=True, vmem_limit_bytes=67043328
        ),
    )(low_feats, mid_feats, high_feats, w_low, w_mid, w_high, norm_gain[None, :], pack, pick)


def solution(mesh):
    in_specs = (
        P("grp", "tp"),
        P("grp", "tp"),
        P("grp", "tp"),
        P("tp", "grp"),
        P("tp", "grp"),
        P("tp", "grp"),
        P("grp"),
        P(),
        P(),
    )
    return jax.shard_map(
        functools.partial(per_device, mesh.shape["grp"], mesh.shape["tp"]),
        mesh=mesh,
        in_specs=in_specs,
        out_specs=P("tp", "grp"),
        check_vma=False,
    )
```

```python
import functools

import jax
import jax.numpy as jnp
from jax import lax
from jax.experimental import pallas as pl
from jax.experimental.pallas import tpu as pltpu
from jax.sharding import PartitionSpec as P

ROWS_G = 8
POS = 6
CAPACITY = 4 * ROWS_G
BATCHES = 2
SLOTS = CAPACITY // BATCHES
LAYERS = 3
STEPS = BATCHES * LAYERS
AHEAD = 2
TILE = 256
EPSILON = 1e-05


def kernel(
    groups, owners,
    low_ref, mid_ref, high_ref, w_low, w_mid, w_high, gain_ref, accepted_ref, assignment_ref,
    out_ref,
    feats, weights, blocks, sums, parts, squares, rows_out, pick,
    f_sem, w_sem, send_sem, recv_sem, part_send, part_recv, sq_send, sq_recv, row_send, row_recv,
):
    me = lax.axis_index("grp")
    own = lax.axis_index("tp")
    chip, core = me // 2, me % 2
    chips = groups // 2
    sibling = chip * 2 + 1 - core
    columns = sums.shape[2]
    share = rows_out.shape[2]
    width = groups * columns
    tiles = columns // TILE
    tokens = feats.shape[1]
    slab = out_ref.shape[0]
    pair_slots = 2 * CAPACITY // ROWS_G

    reads = [
        pltpu.make_async_copy(f, feats.at[i], f_sem.at[i])
        for i, f in enumerate((low_ref, mid_ref, high_ref))
    ]
    for read in reads:
        read.start()
    loads = [
        pltpu.make_async_copy(w, weights.at[i], w_sem.at[i])
        for i, w in enumerate((w_low, w_mid, w_high))
    ]

    barrier = pltpu.get_barrier_semaphore()
    for d in range(1, groups):
        pl.semaphore_signal(
            barrier, inc=1, device_id={"grp": lax.rem(me + d, groups)},
            device_id_type=pl.DeviceIdType.MESH,
        )
    for d in range(1, owners):
        pl.semaphore_signal(
            barrier, inc=1, device_id={"tp": lax.rem(own + d, owners)},
            device_id_type=pl.DeviceIdType.MESH,
        )

    def rows_of(group):
        return pl.ds(pl.multiple_of(group * SLOTS, SLOTS), SLOTS)

    slot = lax.broadcasted_iota(jnp.int32, (CAPACITY, tokens), 0)
    token = lax.broadcasted_iota(jnp.int32, (CAPACITY, tokens), 1)
    packing = jnp.zeros((CAPACITY, tokens), jnp.float32)
    for k in range(ROWS_G):
        count = accepted_ref[me * ROWS_G + k] + 1
        start = (k // 2) * pair_slots
        if k % 2 == 1:
            start = start + accepted_ref[me * ROWS_G + k - 1] + 1
        position = token - k * POS
        hit = (position >= 0) & (position < count) & (slot == start + position)
        packing = jnp.where(hit, 1.0, packing)
    packing = packing.astype(jnp.bfloat16)

    def pack(layer):
        reads[layer].wait()
        packed = jnp.dot(packing, feats[layer], preferred_element_type=jnp.float32)
        for b in range(BATCHES):
            blocks[b * LAYERS + layer, rows_of(me), :] = packed[
                b * SLOTS : (b + 1) * SLOTS
            ].astype(jnp.bfloat16)

    pack(0)
    pl.semaphore_wait(barrier, groups + owners - 2)

    def block_copy(way, step, group):
        target = (chip * 2 + 2 + core, chip * 2 - 2 + core, sibling)[way]
        return pltpu.make_async_remote_copy(
            src_ref=blocks.at[step, rows_of(group), :],
            dst_ref=blocks.at[step, rows_of(group), :],
            send_sem=send_sem.at[way, step, group // 2],
            recv_sem=recv_sem.at[step, group],
            device_id={"grp": target},
            device_id_type=pl.DeviceIdType.MESH,
        )

    def send_own(step):
        @pl.when(chip < chips - 1)
        def _():
            block_copy(0, step, me).start()

        @pl.when(chip > 0)
        def _():
            block_copy(1, step, me).start()

        block_copy(2, step, me).start()

    def relay(step, d):
        @pl.when(chip - d >= 0)
        def _():
            group = me - 2 * d
            block_copy(0, step, group).wait_recv()

            @pl.when(chip < chips - 1)
            def _():
                block_copy(0, step, group).start()

            block_copy(2, step, group).start()

        @pl.when(chip + d <= chips - 1)
        def _():
            group = me + 2 * d
            block_copy(1, step, group).wait_recv()

            @pl.when(chip > 0)
            def _():
                block_copy(1, step, group).start()

            block_copy(2, step, group).start()

    def relays(step, first, last):
        @pl.loop(first, last)
        def _(d):
            relay(step, d)

    def arrive(step):
        for q in range(chips):
            block_copy(2, step, q * 2 + 1 - core).wait_recv()

    def multiply(step):
        b, layer = step // LAYERS, step % LAYERS

        @pl.loop(0, tiles)
        def _(j):
            cols = pl.ds(pl.multiple_of(j * TILE, TILE), TILE)
            product = jnp.dot(
                blocks[step], weights[layer, :, cols], preferred_element_type=jnp.float32
            )
            if layer == 0:
                sums[b, :, cols] = product
            else:
                sums[b, :, cols] += product
            if layer == LAYERS - 1:
                for d in range(1, owners):
                    part_copy(b, d, j).start()
            if step + 1 < STEPS:
                relays(
                    step + 1,
                    1 + (chips - 1) * j // tiles,
                    1 + (chips - 1) * (j + 1) // tiles,
                )
            if b > 0 and layer == 1:
                @pl.when(j == tiles // 2)
                def _():
                    reduce(b - 1)

    def share_of(owner):
        return pl.ds(pl.multiple_of(owner * share, share), share)

    def part_copy(b, d, j):
        cols = pl.ds(pl.multiple_of(j * TILE, TILE), TILE)
        target = lax.rem(own + d, owners)
        return pltpu.make_async_remote_copy(
            src_ref=sums.at[b, share_of(target), cols],
            dst_ref=parts.at[b, d - 1, :, cols],
            send_sem=part_send.at[b, d - 1, j],
            recv_sem=part_recv.at[b, d - 1, j],
            device_id={"tp": target},
            device_id_type=pl.DeviceIdType.MESH,
        )

    def square_copy(b, d):
        return pltpu.make_async_remote_copy(
            src_ref=squares.at[b, 0],
            dst_ref=squares.at[b, d],
            send_sem=sq_send.at[b, d - 1],
            recv_sem=sq_recv.at[b, d - 1],
            device_id={"grp": lax.rem(me + d, groups)},
            device_id_type=pl.DeviceIdType.MESH,
        )

    def row_copy(b, d):
        return pltpu.make_async_remote_copy(
            src_ref=rows_out.at[b, own],
            dst_ref=rows_out.at[b, own],
            send_sem=row_send.at[b, d - 1],
            recv_sem=row_recv.at[b, d - 1],
            device_id={"tp": lax.rem(own + d, owners)},
            device_id_type=pl.DeviceIdType.MESH,
        )

    diagonal = lax.broadcasted_iota(jnp.int32, (share, 128), 0) == lax.broadcasted_iota(
        jnp.int32, (share, 128), 1
    )

    def reduce(b):
        def body(j, square):
            cols = pl.ds(pl.multiple_of(j * TILE, TILE), TILE)
            total = sums[b, share_of(own), cols]
            for d in range(1, owners):
                part_copy(b, d, j).wait_recv()
                total = total + parts[b, d - 1, :, cols]
            parts[b, owners - 1, :, cols] = total
            return square + jnp.sum(total * total, axis=1, keepdims=True)

        square = lax.fori_loop(0, tiles, body, jnp.zeros((share, 1), jnp.float32))
        lanes = jnp.sum(jnp.where(diagonal, square, 0.0), axis=0, keepdims=True)
        squares[b, 0] = jnp.broadcast_to(lanes, (8, 128))
        for d in range(1, groups):
            square_copy(b, d).start()

    def finish(b):
        for d in range(1, groups):
            square_copy(b, d).wait_recv()
        lanes = squares[b, 0]
        for d in range(1, groups):
            lanes = lanes + squares[b, d]
        square = jnp.sum(jnp.where(diagonal, lanes[0:1], 0.0), axis=1, keepdims=True)
        inverse = lax.rsqrt(square / width + EPSILON)
        rows_out[b, own] = (parts[b, owners - 1] * inverse * gain_ref[...]).astype(jnp.bfloat16)
        for d in range(1, owners):
            row_copy(b, d).start()

    send_own(0)
    pack(1)
    send_own(1)
    for load in loads:
        load.start()
    pack(2)

    column = lax.broadcasted_iota(jnp.int32, pick.shape, 1)
    batch_rows = groups * SLOTS
    batch_bits, slot_bits = batch_rows.bit_length() - 1, SLOTS.bit_length() - 1
    group_of = lax.shift_right_logical(column & (batch_rows - 1), slot_bits)
    slot_of = lax.shift_right_logical(column, batch_bits) * SLOTS + (column & (SLOTS - 1))
    place = group_of * CAPACITY + slot_of
    line = lax.broadcasted_iota(jnp.int32, pick.shape, 0)
    picking = jnp.zeros(pick.shape, jnp.float32)
    for k in range(slab // POS):
        source = assignment_ref[own * (slab // POS) + k]
        count = accepted_ref[source] + 1
        local = source & (ROWS_G - 1)
        odd = local & 1
        before = (accepted_ref[jnp.maximum(source - 1, 0)] + 1) * odd
        start = (source - local) // ROWS_G * CAPACITY + (local - odd) // 2 * pair_slots + before
        position = line - k * POS
        hit = (position >= 0) & (position < count) & (place == start + position)
        picking = jnp.where(hit, 1.0, picking)
    pick[...] = picking.astype(jnp.bfloat16)

    relays(0, 1, chips)
    arrive(0)
    for step in range(STEPS):
        if step + AHEAD < STEPS:
            send_own(step + AHEAD)
        if step < LAYERS:
            loads[step].wait()
        multiply(step)
        if step + 1 < STEPS:
            arrive(step + 1)
        if step >= LAYERS and step % LAYERS == 1:
            finish(step // LAYERS - 1)
    reduce(BATCHES - 1)
    finish(BATCHES - 1)
    for b in range(BATCHES):
        for d in range(1, owners):
            row_copy(b, d).wait_recv()

    everything = rows_out[...].reshape(BATCHES * owners * share, columns)
    out_ref[...] = jnp.dot(
        pick[...], everything, preferred_element_type=jnp.float32
    ).astype(jnp.bfloat16)

    for step in range(STEPS):
        for q in range(chips):
            group = q * 2 + core

            @pl.when((chip < chips - 1) & (q <= chip))
            def _():
                block_copy(0, step, group).wait_send()

            @pl.when((chip > 0) & (q >= chip))
            def _():
                block_copy(1, step, group).wait_send()

            block_copy(2, step, group).wait_send()
    for b in range(BATCHES):
        for d in range(1, owners):
            @pl.loop(0, tiles)
            def _(j):
                part_copy(b, d, j).wait_send()

            row_copy(b, d).wait_send()
        for d in range(1, groups):
            square_copy(b, d).wait_send()


def per_device(
    groups, owners,
    low_feats, mid_feats, high_feats, w_low, w_mid, w_high, norm_gain, accepted, assignment,
):
    tokens, depth = low_feats.shape
    columns = w_low.shape[1]
    rows = accepted.shape[0]
    batch_rows = groups * SLOTS
    share = batch_rows // owners
    slab = rows * POS // owners

    vmem = pl.BlockSpec(memory_space=pltpu.VMEM)
    hbm = pl.BlockSpec(memory_space=pl.ANY)
    smem = pl.BlockSpec(memory_space=pltpu.SMEM)
    dma = pltpu.SemaphoreType.DMA
    return pl.pallas_call(
        functools.partial(kernel, groups, owners),
        out_shape=jax.ShapeDtypeStruct((slab, columns), jnp.bfloat16),
        in_specs=[hbm] * 6 + [vmem] + [smem] * 2,
        out_specs=vmem,
        scratch_shapes=[
            pltpu.VMEM((LAYERS, tokens, depth), jnp.bfloat16),
            pltpu.VMEM((LAYERS, depth, columns), jnp.bfloat16),
            pltpu.VMEM((STEPS, batch_rows, depth), jnp.bfloat16),
            pltpu.VMEM((BATCHES, batch_rows, columns), jnp.float32),
            pltpu.VMEM((BATCHES, owners, share, columns), jnp.float32),
            pltpu.VMEM((BATCHES, groups, 8, 128), jnp.float32),
            pltpu.VMEM((BATCHES, owners, share, columns), jnp.bfloat16),
            pltpu.VMEM((slab, BATCHES * batch_rows), jnp.bfloat16),
            dma((LAYERS,)),
            dma((LAYERS,)),
            dma((3, STEPS, groups // 2)),
            dma((STEPS, groups)),
            dma((BATCHES, owners - 1, columns // TILE)),
            dma((BATCHES, owners - 1, columns // TILE)),
            dma((BATCHES, groups - 1)),
            dma((BATCHES, groups - 1)),
            dma((BATCHES, owners - 1)),
            dma((BATCHES, owners - 1)),
        ],
        compiler_params=pltpu.CompilerParams(
            collective_id=0, has_side_effects=True, vmem_limit_bytes=67043328
        ),
    )(low_feats, mid_feats, high_feats, w_low, w_mid, w_high, norm_gain[None, :], accepted, assignment)


def solution(mesh):
    in_specs = (
        P("grp", "tp"),
        P("grp", "tp"),
        P("grp", "tp"),
        P("tp", "grp"),
        P("tp", "grp"),
        P("tp", "grp"),
        P("grp"),
        P(),
        P(),
    )
    return jax.shard_map(
        functools.partial(per_device, mesh.shape["grp"], mesh.shape["tp"]),
        mesh=mesh,
        in_specs=in_specs,
        out_specs=P("tp", "grp"),
        check_vma=False,
    )
```

```python
import functools

import jax
import jax.numpy as jnp
from jax import lax
from jax.experimental import pallas as pl
from jax.experimental.pallas import tpu as pltpu
from jax.sharding import PartitionSpec as P

ROWS_G = 8
POS = 6
CAPACITY = 4 * ROWS_G
BATCHES = 2
SLOTS = CAPACITY // BATCHES
LAYERS = 3
STEPS = BATCHES * LAYERS
AHEAD = 2
TILE = 256
PIECES = 1
EPSILON = 1e-05


def kernel(
    groups, owners,
    low_ref, mid_ref, high_ref, w_low, w_mid, w_high, gain_ref, accepted_ref, assignment_ref,
    out_ref,
    feats, weights, blocks, sums, parts, squares, rows_out, pick,
    f_sem, w_sem, send_sem, recv_sem, part_send, part_recv, sq_send, sq_recv, row_send, row_recv,
):
    me = lax.axis_index("grp")
    own = lax.axis_index("tp")
    chip, core = me // 2, me % 2
    chips = groups // 2
    sibling = chip * 2 + 1 - core
    columns = sums.shape[2]
    share = rows_out.shape[2]
    width = groups * columns
    tiles = columns // TILE
    tokens = feats.shape[1]
    slab = out_ref.shape[0]
    pair_slots = 2 * CAPACITY // ROWS_G

    reads = [
        pltpu.make_async_copy(f, feats.at[i], f_sem.at[i])
        for i, f in enumerate((low_ref, mid_ref, high_ref))
    ]
    for read in reads:
        read.start()
    loads = [
        pltpu.make_async_copy(w, weights.at[i], w_sem.at[i])
        for i, w in enumerate((w_low, w_mid, w_high))
    ]

    barrier = pltpu.get_barrier_semaphore()
    for d in range(1, groups):
        pl.semaphore_signal(
            barrier, inc=1, device_id={"grp": lax.rem(me + d, groups)},
            device_id_type=pl.DeviceIdType.MESH,
        )
    for d in range(1, owners):
        pl.semaphore_signal(
            barrier, inc=1, device_id={"tp": lax.rem(own + d, owners)},
            device_id_type=pl.DeviceIdType.MESH,
        )

    def rows_of(group):
        return pl.ds(pl.multiple_of(group * SLOTS, SLOTS), SLOTS)

    slot = lax.broadcasted_iota(jnp.int32, (CAPACITY, tokens), 0)
    token = lax.broadcasted_iota(jnp.int32, (CAPACITY, tokens), 1)
    packing = jnp.zeros((CAPACITY, tokens), jnp.float32)
    for k in range(ROWS_G):
        count = accepted_ref[me * ROWS_G + k] + 1
        start = (k // 2) * pair_slots
        if k % 2 == 1:
            start = start + accepted_ref[me * ROWS_G + k - 1] + 1
        position = token - k * POS
        hit = (position >= 0) & (position < count) & (slot == start + position)
        packing = jnp.where(hit, 1.0, packing)
    packing = packing.astype(jnp.bfloat16)

    def pack(layer):
        reads[layer].wait()
        packed = jnp.dot(packing, feats[layer], preferred_element_type=jnp.float32)
        for b in range(BATCHES):
            blocks[b * LAYERS + layer, rows_of(me), :] = packed[
                b * SLOTS : (b + 1) * SLOTS
            ].astype(jnp.bfloat16)

    pack(0)
    pl.semaphore_wait(barrier, groups + owners - 2)

    def block_copy(way, step, group):
        target = (chip * 2 + 2 + core, chip * 2 - 2 + core, sibling)[way]
        return pltpu.make_async_remote_copy(
            src_ref=blocks.at[step, rows_of(group), :],
            dst_ref=blocks.at[step, rows_of(group), :],
            send_sem=send_sem.at[way, step, group // 2],
            recv_sem=recv_sem.at[step, group],
            device_id={"grp": target},
            device_id_type=pl.DeviceIdType.MESH,
        )

    def send_own(step):
        @pl.when(chip < chips - 1)
        def _():
            block_copy(0, step, me).start()

        @pl.when(chip > 0)
        def _():
            block_copy(1, step, me).start()

        block_copy(2, step, me).start()

    def relay(step, d):
        @pl.when(chip - d >= 0)
        def _():
            group = me - 2 * d
            block_copy(0, step, group).wait_recv()

            @pl.when(chip < chips - 1)
            def _():
                block_copy(0, step, group).start()

            block_copy(2, step, group).start()

        @pl.when(chip + d <= chips - 1)
        def _():
            group = me + 2 * d
            block_copy(1, step, group).wait_recv()

            @pl.when(chip > 0)
            def _():
                block_copy(1, step, group).start()

            block_copy(2, step, group).start()

    def relays(step, first, last):
        @pl.loop(first, last)
        def _(d):
            relay(step, d)

    def arrive(step):
        for q in range(chips):
            block_copy(2, step, q * 2 + 1 - core).wait_recv()

    def multiply(step):
        b, layer = step // LAYERS, step % LAYERS

        @pl.loop(0, tiles)
        def _(j):
            cols = pl.ds(pl.multiple_of(j * TILE, TILE), TILE)
            product = jnp.dot(
                blocks[step], weights[layer, :, cols], preferred_element_type=jnp.float32
            )
            if layer == 0:
                sums[b, :, cols] = product
            else:
                sums[b, :, cols] += product
            if layer == LAYERS - 1:
                @pl.when(j % piece_tiles == piece_tiles - 1)
                def _():
                    for d in range(1, owners):
                        part_copy(b, d, j // piece_tiles).start()

            if step + 1 < STEPS:
                relays(
                    step + 1,
                    1 + (chips - 1) * j // tiles,
                    1 + (chips - 1) * (j + 1) // tiles,
                )
            if b > 0 and layer == 1:
                @pl.when(j == tiles // 2)
                def _():
                    reduce(b - 1)

    def share_of(owner):
        return pl.ds(pl.multiple_of(owner * share, share), share)

    piece = columns // PIECES
    piece_tiles = tiles // PIECES

    def part_copy(b, d, h):
        cols = pl.ds(pl.multiple_of(h * piece, piece), piece)
        target = lax.rem(own + d, owners)
        return pltpu.make_async_remote_copy(
            src_ref=sums.at[b, share_of(target), cols],
            dst_ref=parts.at[b, d - 1, :, cols],
            send_sem=part_send.at[b, d - 1, h],
            recv_sem=part_recv.at[b, d - 1, h],
            device_id={"tp": target},
            device_id_type=pl.DeviceIdType.MESH,
        )

    def square_copy(b, d):
        return pltpu.make_async_remote_copy(
            src_ref=squares.at[b, 0],
            dst_ref=squares.at[b, d],
            send_sem=sq_send.at[b, d - 1],
            recv_sem=sq_recv.at[b, d - 1],
            device_id={"grp": lax.rem(me + d, groups)},
            device_id_type=pl.DeviceIdType.MESH,
        )

    def row_copy(b, d):
        return pltpu.make_async_remote_copy(
            src_ref=rows_out.at[b, own],
            dst_ref=rows_out.at[b, own],
            send_sem=row_send.at[b, d - 1],
            recv_sem=row_recv.at[b, d - 1],
            device_id={"tp": lax.rem(own + d, owners)},
            device_id_type=pl.DeviceIdType.MESH,
        )

    diagonal = lax.broadcasted_iota(jnp.int32, (share, 128), 0) == lax.broadcasted_iota(
        jnp.int32, (share, 128), 1
    )

    def reduce(b):
        def body(h, square):
            cols = pl.ds(pl.multiple_of(h * piece, piece), piece)
            total = sums[b, share_of(own), cols]
            for d in range(1, owners):
                part_copy(b, d, h).wait_recv()
                total = total + parts[b, d - 1, :, cols]
            parts[b, owners - 1, :, cols] = total
            return square + jnp.sum(total * total, axis=1, keepdims=True)

        square = lax.fori_loop(0, PIECES, body, jnp.zeros((share, 1), jnp.float32))
        lanes = jnp.sum(jnp.where(diagonal, square, 0.0), axis=0, keepdims=True)
        squares[b, 0] = jnp.broadcast_to(lanes, (8, 128))
        for d in range(1, groups):
            square_copy(b, d).start()

    def finish(b):
        for d in range(1, groups):
            square_copy(b, d).wait_recv()
        lanes = squares[b, 0]
        for d in range(1, groups):
            lanes = lanes + squares[b, d]
        square = jnp.sum(jnp.where(diagonal, lanes[0:1], 0.0), axis=1, keepdims=True)
        inverse = lax.rsqrt(square / width + EPSILON)
        rows_out[b, own] = (parts[b, owners - 1] * inverse * gain_ref[...]).astype(jnp.bfloat16)
        for d in range(1, owners):
            row_copy(b, d).start()

    send_own(0)
    pack(1)
    send_own(1)
    for load in loads:
        load.start()
    pack(2)

    column = lax.broadcasted_iota(jnp.int32, pick.shape, 1)
    batch_rows = groups * SLOTS
    batch_bits, slot_bits = batch_rows.bit_length() - 1, SLOTS.bit_length() - 1
    group_of = lax.shift_right_logical(column & (batch_rows - 1), slot_bits)
    slot_of = lax.shift_right_logical(column, batch_bits) * SLOTS + (column & (SLOTS - 1))
    place = group_of * CAPACITY + slot_of
    line = lax.broadcasted_iota(jnp.int32, pick.shape, 0)
    picking = jnp.zeros(pick.shape, jnp.float32)
    for k in range(slab // POS):
        source = assignment_ref[own * (slab // POS) + k]
        count = accepted_ref[source] + 1
        local = source & (ROWS_G - 1)
        odd = local & 1
        before = (accepted_ref[jnp.maximum(source - 1, 0)] + 1) * odd
        start = (source - local) // ROWS_G * CAPACITY + (local - odd) // 2 * pair_slots + before
        position = line - k * POS
        hit = (position >= 0) & (position < count) & (place == start + position)
        picking = jnp.where(hit, 1.0, picking)
    pick[...] = picking.astype(jnp.bfloat16)

    relays(0, 1, chips)
    arrive(0)
    for step in range(STEPS):
        if step + AHEAD < STEPS:
            send_own(step + AHEAD)
        if step < LAYERS:
            loads[step].wait()
        multiply(step)
        if step + 1 < STEPS:
            arrive(step + 1)
        if step >= LAYERS and step % LAYERS == 2:
            finish(step // LAYERS - 1)
    reduce(BATCHES - 1)
    finish(BATCHES - 1)
    for b in range(BATCHES):
        for d in range(1, owners):
            row_copy(b, d).wait_recv()

    everything = rows_out[...].reshape(BATCHES * owners * share, columns)
    out_ref[...] = jnp.dot(
        pick[...], everything, preferred_element_type=jnp.float32
    ).astype(jnp.bfloat16)

    for step in range(STEPS):
        for q in range(chips):
            group = q * 2 + core

            @pl.when((chip < chips - 1) & (q <= chip))
            def _():
                block_copy(0, step, group).wait_send()

            @pl.when((chip > 0) & (q >= chip))
            def _():
                block_copy(1, step, group).wait_send()

            block_copy(2, step, group).wait_send()
    for b in range(BATCHES):
        for d in range(1, owners):
            for h in range(PIECES):
                part_copy(b, d, h).wait_send()
            row_copy(b, d).wait_send()
        for d in range(1, groups):
            square_copy(b, d).wait_send()


def per_device(
    groups, owners,
    low_feats, mid_feats, high_feats, w_low, w_mid, w_high, norm_gain, accepted, assignment,
):
    tokens, depth = low_feats.shape
    columns = w_low.shape[1]
    rows = accepted.shape[0]
    batch_rows = groups * SLOTS
    share = batch_rows // owners
    slab = rows * POS // owners

    vmem = pl.BlockSpec(memory_space=pltpu.VMEM)
    hbm = pl.BlockSpec(memory_space=pl.ANY)
    smem = pl.BlockSpec(memory_space=pltpu.SMEM)
    dma = pltpu.SemaphoreType.DMA
    return pl.pallas_call(
        functools.partial(kernel, groups, owners),
        out_shape=jax.ShapeDtypeStruct((slab, columns), jnp.bfloat16),
        in_specs=[hbm] * 6 + [vmem] + [smem] * 2,
        out_specs=vmem,
        scratch_shapes=[
            pltpu.VMEM((LAYERS, tokens, depth), jnp.bfloat16),
            pltpu.VMEM((LAYERS, depth, columns), jnp.bfloat16),
            pltpu.VMEM((STEPS, batch_rows, depth), jnp.bfloat16),
            pltpu.VMEM((BATCHES, batch_rows, columns), jnp.float32),
            pltpu.VMEM((BATCHES, owners, share, columns), jnp.float32),
            pltpu.VMEM((BATCHES, groups, 8, 128), jnp.float32),
            pltpu.VMEM((BATCHES, owners, share, columns), jnp.bfloat16),
            pltpu.VMEM((slab, BATCHES * batch_rows), jnp.bfloat16),
            dma((LAYERS,)),
            dma((LAYERS,)),
            dma((3, STEPS, groups // 2)),
            dma((STEPS, groups)),
            dma((BATCHES, owners - 1, PIECES)),
            dma((BATCHES, owners - 1, PIECES)),
            dma((BATCHES, groups - 1)),
            dma((BATCHES, groups - 1)),
            dma((BATCHES, owners - 1)),
            dma((BATCHES, owners - 1)),
        ],
        compiler_params=pltpu.CompilerParams(
            collective_id=0, has_side_effects=True, vmem_limit_bytes=67043328
        ),
    )(low_feats, mid_feats, high_feats, w_low, w_mid, w_high, norm_gain[None, :], accepted, assignment)


def solution(mesh):
    in_specs = (
        P("grp", "tp"),
        P("grp", "tp"),
        P("grp", "tp"),
        P("tp", "grp"),
        P("tp", "grp"),
        P("tp", "grp"),
        P("grp"),
        P(),
        P(),
    )
    return jax.shard_map(
        functools.partial(per_device, mesh.shape["grp"], mesh.shape["tp"]),
        mesh=mesh,
        in_specs=in_specs,
        out_specs=P("tp", "grp"),
        check_vma=False,
    )
```
